128 devices in a mesh: ctx: 16 (over y, z), head: 8 (over x, core).
Axes of the slice: x: 4, y: 4, z: 4, core: 2. Of those that a mesh axis runs over, the one named last changes fastest.
Arguments:
- prompt_states: bfloat16 [8192, 2048], P('ctx')
- decode_states: bfloat16 [4, 2048], replicated
- lengths: int32 [4], replicated, may hold values from 1 to 4096, 8192 in all
- page_table: int32 [64], replicated, may hold values from 0 to 63, as said below
- w_query: bfloat16 [2048, 3072], P(None, 'head'), may hold values from -0.125 to 0.125
- w_down: bfloat16 [2048, 576], replicated, may hold values from -0.125 to 0.125
- kv_gain: float32 [512], replicated, may hold values from 0.1 to 1.9
- w_up: bfloat16 [512, 4096], P(None, 'head'), may hold values from -0.25 to 0.25
- w_out: bfloat16 [2048, 2048], P('head'), may hold values from -0.125 to 0.125
Outputs:
- prefill_out: bfloat16 [8192, 2048], P(('ctx', 'head'))
- paged_cache: bfloat16 [8192, 576], P('ctx')
- decode_out: bfloat16 [4, 2048], replicated
The draws below stay inside these ranges and needn't reach their ends.
Inputs may be any that keep to these rules, and one draw needn't show every extreme that they name: page_table is a permutation of the 64 pages; the logical pages of ctx index c are c * 4 to c * 4 + 3, and physical page p lies on ctx index p // 4; logical page c * 4 + w has physical page ((c + s_w) mod 16) * 4 + w, where the shifts s_0 to s_(3) are distinct numbers of 0 to 16 - 1, the same for every c.
All inputs are finite; a program needn't handle non-finite values.
Results may differ from the reference program's by a relative error of at most 0.025.
Values may be sent and summed in bfloat16 or wider, within the bound.
No kernel may reach another device: no remote copies, remote signals or barrier semaphores. Data moves between devices by JAX's collectives and lax.ppermute only.
A program may use at most 192 MiB of HBM per device.

```python
import math
import jax
import jax.numpy as jnp
import numpy as np
from jax import lax

D = 2048
HEADS = 16
NOPE = 128
ROPE = 64
VDIM = 128
RANK = 512
PAGE = 128
REQS = 4
TOK_DEV = 512
TOKENS = 8192
PAGES_DEV = 4
PAGES = 64
N_CTX = 16


def rough_states(key, rows):
    return jax.random.normal(key, (rows, D), jnp.float32).astype(jnp.bfloat16)


def draw_prompt_states(key, part):
    return rough_states(jax.random.fold_in(key, 11), TOKENS)


def draw_decode_states(key, part):
    return rough_states(jax.random.fold_in(key, 12), REQS)


def draw_page_table(key, part):
    offsets = jax.random.permutation(jax.random.fold_in(key, 13), N_CTX)[:PAGES_DEV]
    logical = jnp.arange(PAGES, dtype=jnp.int32)
    source = logical // PAGES_DEV
    within = logical % PAGES_DEV
    target = (source + offsets[within]) % N_CTX
    return (target * PAGES_DEV + within).astype(jnp.int32)


def levels(rng, shape, shards, least, top_value):
    level = 1.0
    for axis_at, shards_of in shards:
        draws = jax.random.uniform(jax.random.fold_in(jax.random.fold_in(rng, 6), axis_at), (shards_of,), jnp.float32, least / len(shards), top_value / len(shards))
        level = level * jnp.repeat(jnp.exp(draws), shape[axis_at] // shards_of).reshape((-1,) + (1,) * (len(shape) - 1 - axis_at))
    return level


def profile(number_of, total, most, skew):
    weights = [(1 << 20) // math.isqrt(grade ** skew) + 1 for grade in range(2, number_of + 1)]
    spare, counts = total - most - (number_of - 1), [1] * (number_of - 1)
    while spare > 0:
        free = [i for i in range(number_of - 1) if counts[i] < most]
        whole, left = sum([weights[i] for i in free]), spare
        for i in free:
            addition = min(most - counts[i], max(1, left * weights[i] // whole), spare)
            counts[i] = counts[i] + addition
            spare = spare - addition
    return np.array([most] + counts)


def uneven_parts(stream_key, number_of, total, limit, lean):
    if number_of == 2:
        one = jax.random.randint(stream_key, (), max(1, total - limit), min(limit, total - 1) + 1)
        return jnp.stack([one, total - one])
    tallies = jnp.asarray(profile(number_of, total, limit, lean), jnp.int32)
    couples = (number_of - 1) // 2
    giver, taker = tallies[1:1 + 2 * couples:2], tallies[2:2 + 2 * couples:2]
    room = jnp.minimum(giver - 1, limit - taker)
    moved = jax.random.randint(jax.random.fold_in(stream_key, 1), (couples,), 0, 1 << 20) % (room + 1)
    tallies = tallies.at[1:1 + 2 * couples:2].set(giver - moved).at[2:2 + 2 * couples:2].set(taker + moved)
    return tallies[jax.random.permutation(jax.random.fold_in(stream_key, 2), number_of)]


def noise(key, dims, spread, most, pieces=(), held_as=jnp.bfloat16):
    level = levels(key, dims, pieces, -0.22, 0.18) if pieces else 1.0
    values = jax.random.normal(key, dims, jnp.float32) * spread * level
    return jnp.minimum(jnp.maximum(values, -most), most).astype(held_as)


def setup_inputs(seed: int = 0) -> dict:
    key_of = jax.random.split(jax.random.key(seed), 10)
    return {
        "prompt_states": draw_prompt_states(jax.random.fold_in(key_of[9], 71), 0),
        "decode_states": draw_decode_states(jax.random.fold_in(key_of[9], 71), 0),
        "lengths": uneven_parts(key_of[2], REQS, TOKENS, TOKENS // 2, 2).astype(jnp.int32),
        "page_table": draw_page_table(jax.random.fold_in(key_of[9], 71), 0),
        "w_query": noise(key_of[4], (D, HEADS * (NOPE + ROPE)), D ** -0.5, 0.125, ((1, 8),)),
        "w_down": noise(key_of[5], (D, RANK + ROPE), D ** -0.5, 0.125),
        "kv_gain": jnp.clip(1.0 + 0.18 * jax.random.normal(key_of[6], (RANK,), jnp.float32), 0.1, 1.9),
        "w_up": noise(key_of[7], (RANK, HEADS * (NOPE + VDIM)), RANK ** -0.5, 0.25, ((1, 8),)),
        "w_out": noise(key_of[8], (HEADS * VDIM, D), (HEADS * VDIM) ** -0.5, 0.125, ((0, 8),)),
    }


ROPE_BASE = 50000.0

def rope(vector, place):
    half = vector.shape[-1] // 2
    freq = ROPE_BASE ** (-(jnp.arange(half, dtype=jnp.float32) * 2.0 / vector.shape[-1]))
    angle = place[..., None] * freq
    first, second = (vector[..., :half], vector[..., half:])
    return jnp.concatenate([first * jnp.cos(angle) - second * jnp.sin(angle), first * jnp.sin(angle) + second * jnp.cos(angle)], -1)

def token_info(index, lengths):
    ends = jnp.cumsum(lengths).astype(jnp.int32)
    starts = (ends - lengths).astype(jnp.int32)
    tenant = lax.optimization_barrier(jnp.sum((index[:, None] >= ends[None, :]).astype(jnp.int32), 1)).astype(jnp.int32)
    picked = lax.optimization_barrier(jnp.sum(jnp.where(tenant[:, None] == jnp.arange(lengths.shape[0], dtype=jnp.int32)[None, :], starts[None, :], 0), 1))
    return (tenant, (index - picked).astype(jnp.int32))

def latent_of(states, w_down, kv_gain, place):
    lat = jnp.dot(states, w_down, preferred_element_type=jnp.float32)
    comp = lat[:, :RANK]
    comp = comp * lax.rsqrt(lax.optimization_barrier(jnp.mean(comp * comp, -1, keepdims=True)) + 1e-06) * kv_gain
    return jnp.concatenate([comp, rope(lat[:, RANK:], place)], 1).astype(jnp.bfloat16)

def queries(states, w_query, w_up, place):
    rows = states.shape[0]
    heads = w_query.shape[1] // (NOPE + ROPE)
    qfull = jnp.dot(states, w_query, preferred_element_type=jnp.float32).astype(jnp.bfloat16).reshape(rows, heads, NOPE + ROPE)
    w_key = w_up.reshape(RANK, heads, NOPE + VDIM)[:, :, :NOPE]
    qnope = jnp.einsum('thn,rhn->thr', qfull[..., :NOPE].astype(jnp.float32), w_key.astype(jnp.float32))
    qrope = rope(qfull[..., NOPE:].astype(jnp.float32), place[:, None])
    scale = (NOPE + ROPE) ** (-0.5)
    return (jnp.concatenate([qnope, qrope], -1) * scale).astype(jnp.bfloat16)

def values_of(mixed, w_up):
    heads = w_up.shape[1] // (NOPE + VDIM)
    w_val = w_up.reshape(RANK, heads, NOPE + VDIM)[:, :, NOPE:]
    out = jnp.einsum('thr,rhv->thv', mixed.astype(jnp.float32), w_val.astype(jnp.float32))
    return out.astype(jnp.bfloat16).reshape(mixed.shape[0], heads * VDIM)

def reference(prompt_states, decode_states, lengths, page_table, w_query, w_down, kv_gain, w_up, w_out):
    index = jnp.arange(TOKENS, dtype=jnp.int32)
    tenant, place = token_info(index, lengths)
    latent = latent_of(prompt_states, w_down, kv_gain, place.astype(jnp.float32))
    query = queries(prompt_states, w_query, w_up, place.astype(jnp.float32))
    keys = latent.astype(jnp.float32)

    def block(item):
        qblock, iblock, tblock = item
        score = jnp.einsum('thk,uk->thu', qblock.astype(jnp.float32), keys)
        mask = (tenant[None, :] == tblock[:, None]) & (index[None, :] <= iblock[:, None])
        score = jnp.where(mask[:, None, :], score, -jnp.inf)
        top = lax.optimization_barrier(jnp.max(score, -1, keepdims=True))
        prob = jnp.where(mask[:, None, :], jnp.exp(score - top), 0.0)
        total = lax.optimization_barrier(jnp.sum(prob, -1))
        acc = jnp.einsum('thu,ur->thr', prob.astype(jnp.bfloat16).astype(jnp.float32), keys[:, :RANK])
        return (acc / total[..., None]).astype(jnp.bfloat16)
    mixed = lax.map(block, (query.reshape(N_CTX, TOK_DEV, HEADS, RANK + ROPE), index.reshape(N_CTX, TOK_DEV), tenant.reshape(N_CTX, TOK_DEV)))
    mixed = mixed.reshape(TOKENS, HEADS, RANK)
    heads_out = values_of(mixed, w_up)
    prefill_out = jnp.dot(heads_out, w_out, preferred_element_type=jnp.float32).astype(jnp.bfloat16)
    rows = (page_table[:, None] * PAGE + jnp.arange(PAGE, dtype=jnp.int32)[None, :]).reshape(-1).astype(jnp.int32)
    paged_cache = jnp.zeros((TOKENS, RANK + ROPE), jnp.bfloat16).at[rows].set(latent)
    dplace = lengths.astype(jnp.float32)
    new_key = latent_of(decode_states, w_down, kv_gain, dplace)
    dquery = queries(decode_states, w_query, w_up, dplace).astype(jnp.float32)
    score = jnp.einsum('qhk,uk->qhu', dquery, keys)
    dmask = tenant[None, :] == jnp.arange(REQS, dtype=jnp.int32)[:, None]
    score = jnp.where(dmask[:, None, :], score, -jnp.inf)
    own = jnp.einsum('qhk,qk->qh', dquery, new_key.astype(jnp.float32))
    top = jnp.maximum(lax.optimization_barrier(jnp.max(score, -1)), own)
    prob = jnp.where(dmask[:, None, :], jnp.exp(score - top[..., None]), 0.0)
    pown = jnp.exp(own - top)
    total = lax.optimization_barrier(jnp.sum(prob, -1)) + pown
    acc = jnp.einsum('qhu,ur->qhr', prob.astype(jnp.bfloat16).astype(jnp.float32), keys[:, :RANK])
    acc = acc + pown.astype(jnp.bfloat16).astype(jnp.float32)[..., None] * new_key[:, None, :RANK].astype(jnp.float32)
    dmixed = (acc / total[..., None]).astype(jnp.bfloat16)
    dheads = values_of(dmixed, w_up)
    decode_out = jnp.dot(dheads, w_out, preferred_element_type=jnp.float32).astype(jnp.bfloat16)
    return (prefill_out, paged_cache, decode_out)
```

```python
import functools
import math

import jax
import jax.numpy as jnp
import numpy as np
from jax import lax
from jax.experimental import pallas as pl
from jax.experimental.pallas import tpu as pltpu
from jax.sharding import PartitionSpec as P

NOPE = 128
ROPE = 64
VDIM = 128
RANK = 512
PAGE = 128
PAGES_DEV = 4
ROPE_BASE = 50000.0
HIDDEN = -3e38
FLOOR = -1e30
KAPPA = (NOPE + ROPE) ** -0.5 * math.log2(math.e)
DIST = (1, 3, 2, 4)
FREQ = (
    ROPE_BASE ** (-(np.arange(ROPE // 2, dtype=np.float64) * 2.0 / ROPE))
).astype(np.float32)[:, None]
ATTEND_MIB = {"first": 14, "middle": 16, "last": 16}
EXTRA = 8

F32 = jnp.float32
BF16 = jnp.bfloat16
NT = (((1,), (1,)), ((), ()))


def whole():
    return pl.BlockSpec()


def smem():
    return pl.BlockSpec(memory_space=pltpu.SMEM)


def anywhere():
    return pl.BlockSpec(memory_space=pl.ANY)


def in_hbm(x):
    return pltpu.with_memory_space_constraint(x, pltpu.HBM)


def params(mib):
    return pltpu.CompilerParams(vmem_limit_bytes=mib << 20)


def place_of():
    head = lax.axis_index("head")
    return lax.axis_index("ctx"), head // 2, lax.rem(head, 2)


def back_of(chip):
    chip = lax.rem(chip, 4)
    return jnp.where(chip == 0, 1, jnp.where(chip == 1, 3, jnp.where(chip == 2, 2, 4)))


GROUPS = RANK // 128


def tokens_of(ref):
    return ref.shape[0] * 128 // (RANK + ROPE)


def latent_rows(ref):
    n = tokens_of(ref)
    return jnp.concatenate([ref[g * n : (g + 1) * n, :] for g in range(GROUPS)], 1)


def rotary_rows(ref):
    both = ref[GROUPS * tokens_of(ref) :, :]
    return jnp.concatenate([both[:, :ROPE], both[:, ROPE:]], 0)


def ends_of(lengths):
    e0 = lengths[0]
    e1 = e0 + lengths[1]
    return e0, e1, e1 + lengths[2]


def start_of(index, ends):
    e0, e1, e2 = ends
    return jnp.where(
        index >= e2, e2, jnp.where(index >= e1, e1, jnp.where(index >= e0, e0, 0))
    )


def normed(comp, gain):
    return comp * lax.rsqrt(jnp.mean(comp * comp, -1, keepdims=True) + 1e-06) * gain


def turn_table(place, freq):
    angle = freq * place
    cos, sin = jnp.cos(angle), jnp.sin(angle)
    return jnp.concatenate([cos, cos, -sin, sin], 0).T


def turned(v, cs):
    half = ROPE // 2
    other = jnp.concatenate([v[:, half:], v[:, :half]], 1)
    return v * cs[:, :ROPE] + other * cs[:, ROPE:]


def prompt_turns(lengths, freq, first, n):
    index = first + lax.broadcasted_iota(jnp.int32, (1, n), 1)
    place = (index - start_of(index, ends_of(lengths))).astype(F32)
    return turn_table(place, freq)


def latent_kernel(lengths, x, w, gain, freq, out, cs, acc):
    step = pl.program_id(0)
    n = x.shape[0]

    @pl.when(step == 0)
    def _():
        ctx, _, core = place_of()
        cs[...] = prompt_turns(lengths, freq[...], (2 * ctx + core) * n, n)

    part = lax.dot_general(x[...], w[...], NT, preferred_element_type=F32)

    @pl.when(step == 0)
    def _():
        acc[...] = part

    @pl.when(step > 0)
    def _():
        acc[...] += part

    @pl.when(step == pl.num_programs(0) - 1)
    def _():
        comp = normed(acc[:, :RANK], gain[...]).astype(BF16)
        for g in range(GROUPS):
            out[g * n : (g + 1) * n, :] = comp[:, g * 128 : (g + 1) * 128]
        rot = turned(acc[:, RANK:], cs[...]).astype(BF16)
        out[GROUPS * n :, :] = jnp.concatenate([rot[: n // 2], rot[n // 2 :]], 1)


def latent_of(lengths, x, w_down_t, gain):
    tok, d = x.shape
    n = tok // 2
    width = w_down_t.shape[0]
    steps = 2
    return pl.pallas_call(
        latent_kernel,
        name="latent",
        grid=(steps,),
        in_specs=[
            smem(),
            pl.BlockSpec((n, d // steps), lambda i: (lax.rem(lax.axis_index("head"), 2), i)),
            pl.BlockSpec((width, d // steps), lambda i: (0, i)),
            pl.BlockSpec((1, RANK), lambda i: (0, 0)),
            pl.BlockSpec((ROPE // 2, 1), lambda i: (0, 0)),
        ],
        out_specs=pl.BlockSpec((n * width // 128, 128), lambda i: (0, 0)),
        out_shape=jax.ShapeDtypeStruct((n * width // 128, 128), BF16),
        scratch_shapes=[pltpu.VMEM((n, 2 * ROPE), F32), pltpu.VMEM((n, width), F32)],
        compiler_params=params(14),
        cost_estimate=pl.CostEstimate(
            flops=2 * n * d * width, bytes_accessed=4 << 20, transcendentals=0
        ),
    )(lengths, in_hbm(x), in_hbm(w_down_t), gain, FREQ)


def query_kernel(lengths, x, w, freq, _, out, cs, acc):
    step = pl.program_id(0)
    tok = x.shape[0]

    @pl.when(step == 0)
    def _():
        ctx, _, _ = place_of()
        cs[...] = prompt_turns(lengths, freq[...], ctx * tok, tok)

    part = jnp.dot(x[...], w[...], preferred_element_type=F32)

    @pl.when(step == 0)
    def _():
        acc[...] = part

    @pl.when(step > 0)
    def _():
        acc[...] += part

    @pl.when(step == pl.num_programs(0) - 1)
    def _():
        for h in range(2):
            at = h * (NOPE + ROPE)
            out[h, :, :NOPE] = (acc[:, at : at + NOPE] * KAPPA).astype(BF16)
            r = turned(acc[:, at + NOPE : at + NOPE + ROPE], cs[...]) * KAPPA
            out[h, :, NOPE:] = jnp.concatenate([r, jnp.zeros_like(r)], 1).astype(BF16)


def query_of(lengths, x, w_query, after):
    tok, d = x.shape
    width = w_query.shape[1]
    steps = 2
    return pl.pallas_call(
        query_kernel,
        name="query",
        grid=(steps,),
        in_specs=[
            smem(),
            pl.BlockSpec((tok, d // steps), lambda i: (0, i)),
            pl.BlockSpec((d // steps, width), lambda i: (i, 0)),
            pl.BlockSpec((ROPE // 2, 1), lambda i: (0, 0)),
            anywhere(),
        ],
        out_specs=pl.BlockSpec((2, tok, 256), lambda i: (0, 0, 0)),
        out_shape=jax.ShapeDtypeStruct((2, tok, 256), BF16),
        scratch_shapes=[pltpu.VMEM((tok, 2 * ROPE), F32), pltpu.VMEM((tok, width), F32)],
        compiler_params=params(14),
        cost_estimate=pl.CostEstimate(
            flops=1 << 20, bytes_accessed=1 << 16, transcendentals=0
        ),
    )(lengths, in_hbm(x), in_hbm(w_query), FREQ, after)


def decode_kernel(lengths, x, w_query, w_down_t, gain, freq, w_up, half, sib, out, self_out):
    n = tokens_of(half)
    tok = 2 * n
    rows = x.shape[0]
    keys = jnp.concatenate([latent_rows(half), latent_rows(sib)], 0)
    rot = jnp.concatenate([rotary_rows(half), rotary_rows(sib)], 0)
    ctx, _, core = place_of()
    lane = lax.broadcasted_iota(jnp.int32, (1, 128), 1)
    place = jnp.zeros((1, 128), jnp.int32)
    for r in range(rows):
        place = jnp.where(lane == r, lengths[r], place)
    cs = turn_table(place.astype(F32), freq[...])[:rows]
    lat = lax.dot_general(x[...], w_down_t[...], NT, preferred_element_type=F32)
    new_c = normed(lat[:, :RANK], gain[...]).astype(BF16)
    new_k = turned(lat[:, RANK:], cs).astype(BF16)
    q = jnp.dot(x[...], w_query[...], preferred_element_type=F32)
    index = lax.broadcasted_iota(jnp.int32, (rows, tok), 1)
    index = ctx * tok + jnp.where(index < n, index + core * n, index - core * n)
    tenant = sum((index >= e).astype(jnp.int32) for e in ends_of(lengths))
    mask = tenant == lax.broadcasted_iota(jnp.int32, (rows, tok), 0)
    for h in range(2):
        at = h * (NOPE + ROPE)
        wk = w_up[:, h * 256 : h * 256 + NOPE]
        wv = w_up[:, h * 256 + NOPE : h * 256 + 256]
        qn = (q[:, at : at + NOPE] * KAPPA).astype(BF16)
        qa = lax.dot_general(qn, wk, NT, preferred_element_type=F32).astype(BF16)
        qr = (turned(q[:, at + NOPE : at + NOPE + ROPE], cs) * KAPPA).astype(BF16)
        s = lax.dot_general(qa, keys, NT, preferred_element_type=F32)
        s = s + lax.dot_general(qr, rot, NT, preferred_element_type=F32)
        s = jnp.where(mask, s, HIDDEN)
        top = jnp.maximum(jnp.max(s, -1, keepdims=True), FLOOR)
        p = jnp.exp2(s - top)
        total = jnp.sum(p, -1, keepdims=True)
        mixed = jnp.dot(p.astype(BF16), keys, preferred_element_type=F32)
        part = jnp.dot(mixed.astype(BF16), wv, preferred_element_type=F32)
        own = jnp.sum(qa.astype(F32) * new_c.astype(F32), -1, keepdims=True)
        own = own + jnp.sum(qr.astype(F32) * new_k.astype(F32), -1, keepdims=True)
        to = slice(h * rows, h * rows + rows)
        mine = jnp.concatenate(
            [part, jnp.broadcast_to(top, (rows, 64)), jnp.broadcast_to(total, (rows, 64))], 1
        )
        for c in range(out.shape[0] // (2 * rows)):
            at = c * 2 * rows + h * rows
            out[at : at + rows, :] = mine
        self_out[to, :VDIM] = jnp.dot(new_c, wv, preferred_element_type=F32)
        self_out[to, VDIM : VDIM + 64] = jnp.broadcast_to(own, (rows, 64))
        self_out[to, VDIM + 64 :] = jnp.ones((rows, 64), F32)


def decode_partial(copies, lengths, x, w_query, w_down_t, gain, w_up, half, sib):
    rows = x.shape[0]
    return pl.pallas_call(
        decode_kernel,
        name="decode_partial",
        in_specs=[smem()] + [whole()] * 8,
        out_specs=[whole()] * 2,
        out_shape=[
            jax.ShapeDtypeStruct((copies * 2 * rows, 256), F32),
            jax.ShapeDtypeStruct((2 * rows, 256), F32),
        ],
        compiler_params=params(12),
        cost_estimate=pl.CostEstimate(
            flops=1 << 20, bytes_accessed=1 << 16, transcendentals=0
        ),
    )(lengths, x, w_query, w_down_t, gain, FREQ, w_up, half, sib)


def decode_merge_kernel(parts, own, w_out, _, out):
    rows = own.shape[0] // 2
    n = parts.shape[0] // own.shape[0]
    part = [parts[i * 2 * rows : (i + 1) * 2 * rows, :] for i in range(n)] + [own[...]]
    tops = [p[:, VDIM : VDIM + 1] for p in part]
    top = functools.reduce(jnp.maximum, tops)
    ratio = [jnp.exp2(t - top) for t in tops]
    total = sum(r * p[:, VDIM + 64 : VDIM + 65] for r, p in zip(ratio, part))
    acc = sum(r * p[:, :VDIM] for r, p in zip(ratio, part))
    heads = (acc / total).astype(BF16)
    got = jnp.dot(heads[:rows], w_out[:VDIM], preferred_element_type=F32)
    got = got + jnp.dot(heads[rows:], w_out[VDIM:], preferred_element_type=F32)
    out[...] = jnp.concatenate([got, jnp.zeros((EXTRA - rows, got.shape[1]), F32)], 0)


def decode_merge(parts, own, w_out, after):
    return pl.pallas_call(
        decode_merge_kernel,
        name="decode_merge",
        in_specs=[whole()] * 3 + [anywhere()],
        out_specs=whole(),
        out_shape=jax.ShapeDtypeStruct((EXTRA, w_out.shape[1]), F32),
        compiler_params=params(4),
        cost_estimate=pl.CostEstimate(
            flops=2 * 8 * 2048 * 256, bytes_accessed=2 << 20, transcendentals=0
        ),
    )(parts, own, w_out, after)


def attend_kernel(stage, places, lengths, q_own, q_sib, w_own, w_sib, *refs):
    nseg = len(places)
    segs, refs = refs[:nseg], refs[nseg:]
    if stage == "first":
        _, acc_out, rbuf, kbuf, vbuf, sbuf = refs
    elif stage == "middle":
        acc_in, _, acc_out, rbuf, kbuf, vbuf, sbuf = refs
    else:
        acc_in, _, mine, other, rbuf, kbuf, vbuf, sbuf, tile = refs
    tok = q_own.shape[1]
    heads = 4
    ctx, chip, core = place_of()
    base = ctx * tok
    ends = ends_of(lengths)
    row = base + lax.broadcasted_iota(jnp.int32, (tok, 128), 0)
    low = start_of(row, ends)
    blocks = []
    at = 0
    n = tokens_of(segs[0])
    for lat, place in zip(segs, places):
        if place is None:
            back = base + core * n
        else:
            back = base + core * n - (back_of(chip + place[0]) + place[1]) * tok
        rot = rotary_rows(lat)
        rbuf[at : at + n, :] = jnp.concatenate([rot, jnp.zeros_like(rot)], 1)
        blocks.append((lat, at, back, place is None))
        at += n
    ones = jnp.ones((n, 256 - VDIM), BF16)

    def expand(h):
        w = (w_own if h < 2 else w_sib)[:, (h % 2) * 256 : (h % 2) * 256 + 256]
        for lat, at, _, _ in blocks:
            kv = jnp.dot(latent_rows(lat), w, preferred_element_type=F32)
            kbuf[h, at : at + n, :] = kv[:, :NOPE].astype(BF16)
            vbuf[h, at : at + n, :] = kv[:, NOPE:].astype(BF16)

    def scores(h, block, top):
        _, at, back, causal = block
        q = q_own[h] if h < 2 else q_sib[h - 2]
        k = jnp.concatenate([kbuf[h, at : at + n, :], rbuf[at : at + n, :]], 1)
        s = lax.dot_general(q, k, NT, preferred_element_type=F32)
        for g in range(0, n, 128):
            key = back + g + lax.broadcasted_iota(jnp.int32, (1, 128), 1)
            mask = key >= low
            if causal:
                mask = mask & (key <= row)
            piece = jnp.where(mask, s[:, g : g + 128], HIDDEN)
            sbuf[h % 2, :, at + g : at + g + 128] = piece
            top = piece if top is None else jnp.maximum(top, piece)
        return top

    def finish(h, top, acc):
        if stage != "last":
            acc_out[h, :, : VDIM + 64] = acc[:, : VDIM + 64]
            acc_out[h, :, VDIM + 64 :] = jnp.broadcast_to(top, (tok, 64))
            return
        total = acc[:, VDIM:]
        some = total > 0
        safe = jnp.where(some, total, 1.0)
        tile[:, h * VDIM : h * VDIM + VDIM] = acc[:, :VDIM] / safe
        lse = jnp.where(some, top + jnp.log2(safe), HIDDEN)
        lane = lax.broadcasted_iota(jnp.int32, (tok, 128), 1)
        if h == 0:
            tile[:, heads * VDIM :] = lse
        else:
            tile[:, heads * VDIM :] = jnp.where(
                lane // 32 == h, lse, tile[:, heads * VDIM :]
            )

    expand(0)
    tops = None
    for block in blocks:
        tops = scores(0, block, tops)
    for h in range(heads):
        top = jnp.max(tops, -1, keepdims=True)
        tops = None
        if stage == "first":
            top = jnp.maximum(top, FLOOR)
            acc = None
        else:
            before = acc_in[h, :, VDIM + 64 : VDIM + 65]
            top = jnp.maximum(top, before)
            ratio = jnp.exp2(before - top)
            total = acc_in[h, :, VDIM : VDIM + 1] * ratio
            acc = jnp.concatenate(
                [acc_in[h, :, :VDIM] * ratio, jnp.broadcast_to(total, (tok, VDIM))], 1
            )
        if h + 1 < heads:
            expand(h + 1)
        for block in blocks:
            _, at, _, _ = block
            if h + 1 < heads:
                tops = scores(h + 1, block, tops)
            p = jnp.exp2(sbuf[h % 2, :, at : at + n] - top).astype(BF16)
            v = jnp.concatenate([vbuf[h, at : at + n, :], ones], 1)
            got = jnp.dot(p, v, preferred_element_type=F32)
            acc = got if acc is None else acc + got
        finish(h, top, acc)
    if stage == "last":
        part = tok // 8
        for i in range(4):
            to = slice(i * part, (i + 1) * part)
            at = (2 * i + core) * part
            mine[to, :] = tile[pl.ds(pl.multiple_of(at, part), part), :]
            at = (2 * i + 1 - core) * part
            other[to, :] = tile[pl.ds(pl.multiple_of(at, part), part), :]


def attend(stage, lengths, q_own, q_sib, w_own, w_sib, segs, places, state):
    _, tok, _ = q_own.shape
    heads = 4
    keys = tok // 2 * len(places)
    args = [lengths, q_own, q_sib, w_own, w_sib, *segs, *state]
    scratch = [
        pltpu.VMEM((keys, 128), BF16),
        pltpu.VMEM((heads, keys, 128), BF16),
        pltpu.VMEM((heads, keys, 128), BF16),
        pltpu.VMEM((2, tok, keys), F32),
    ]
    if stage == "last":
        width = heads * VDIM + 128
        out_shape = [jax.ShapeDtypeStruct((tok // 2, width), F32)] * 2
        scratch.append(pltpu.VMEM((tok, width), F32))
    else:
        out_shape = [jax.ShapeDtypeStruct((heads, tok, 256), F32)]
    return pl.pallas_call(
        functools.partial(attend_kernel, stage, places),
        name="attend_" + stage,
        in_specs=[smem()] + [whole()] * (len(args) - 2) + [anywhere()],
        out_specs=[whole()] * len(out_shape),
        out_shape=out_shape,
        scratch_shapes=scratch,
        compiler_params=params(ATTEND_MIB[stage]),
        cost_estimate=pl.CostEstimate(
            flops=2 * heads * tok * keys * 1024,
            bytes_accessed=8 << 20,
            transcendentals=heads * tok * keys,
        ),
    )(*args)


def merge_kernel(mine, came, w_own, w_sib, dec, _, out0, out1, out2, out3, heads):
    _, chip, _ = place_of()
    wide = 4 * VDIM
    for h in range(4):
        g = (h + 2) % 4
        la = mine[:, wide + h * 32 : wide + h * 32 + 1]
        lb = came[:, wide + g * 32 : wide + g * 32 + 1]
        top = jnp.maximum(la, lb)
        wa, wb = jnp.exp2(la - top), jnp.exp2(lb - top)
        scale = 1.0 / (wa + wb)
        o = mine[:, h * VDIM : h * VDIM + VDIM] * (wa * scale)
        o = o + came[:, g * VDIM : g * VDIM + VDIM] * (wb * scale)
        heads[:, h * VDIM : h * VDIM + VDIM] = o.astype(BF16)
    quarter = heads.shape[0] // 4
    part = jnp.concatenate(
        [
            heads[pl.ds(pl.multiple_of(lax.rem(chip + i, 4) * quarter, quarter), quarter), :]
            for i in range(4)
        ],
        0,
    )
    got = jnp.dot(part[:, : 2 * VDIM], w_own[...], preferred_element_type=F32)
    got = got + jnp.dot(part[:, 2 * VDIM :], w_sib[...], preferred_element_type=F32)
    for i, out in enumerate((out0, out1, out2, out3)):
        out[:quarter, :] = got[i * quarter : (i + 1) * quarter].astype(out.dtype)
        out[quarter:, :] = dec[...].astype(out.dtype)


def merge_out(mine, came, w_own, w_sib, dec, after):
    rows, d = mine.shape[0], w_own.shape[1]
    shapes = [
        jax.ShapeDtypeStruct((rows // 4 + EXTRA, d), F32 if i == 0 else BF16) for i in range(4)
    ]
    return pl.pallas_call(
        merge_kernel,
        name="merge_out",
        in_specs=[whole()] * 5 + [anywhere()],
        out_specs=[whole()] * 4,
        out_shape=shapes,
        scratch_shapes=[pltpu.VMEM((rows, 4 * VDIM), BF16)],
        compiler_params=params(24),
        cost_estimate=pl.CostEstimate(
            flops=2 * rows * 512 * d, bytes_accessed=5 << 20, transcendentals=0
        ),
    )(mine, came, w_own, w_sib, dec, after)


def sum_kernel(own, a, b, c, out, dec):
    rows = out.shape[0]
    got = own[...] + a[...].astype(F32) + b[...].astype(F32) + c[...].astype(F32)
    out[...] = got[:rows].astype(BF16)
    dec[...] = got[rows:]


def sum_parts(own, a, b, c):
    rows, d = own.shape
    return pl.pallas_call(
        sum_kernel,
        name="sum_parts",
        in_specs=[whole()] * 4,
        out_specs=[whole()] * 2,
        out_shape=[
            jax.ShapeDtypeStruct((rows - EXTRA, d), BF16),
            jax.ShapeDtypeStruct((EXTRA, d), F32),
        ],
        compiler_params=params(16),
        cost_estimate=pl.CostEstimate(
            flops=40_000_000_000, bytes_accessed=2 << 20, transcendentals=0
        ),
    )(own, a, b, c)


SLOT = RANK + PAGE


def shift_of(table, core, i):
    at = lax.div(table[2 * core + i], PAGES_DEV)
    return at


def pages_kernel(table, own, *refs):
    halves, (_, near, far) = refs[:8], refs[8:]
    _, chip, core = place_of()
    held = [(own, 0)]
    for i, half in enumerate(halves):
        held.append((half, back_of(chip + i % 4) + i // 4 * 4))

    def copy(half, i, out):
        n = tokens_of(half)
        for g in range(GROUPS):
            at = g * n + i * PAGE
            out[i * SLOT + g * PAGE : i * SLOT + (g + 1) * PAGE, :] = half[at : at + PAGE, :]
        rot = half[GROUPS * n :, :]
        if i:
            rot = jnp.concatenate([rot[:, ROPE:], rot[:, :ROPE]], 1)
        out[i * SLOT + RANK : (i + 1) * SLOT, :] = rot

    for i in range(PAGES_DEV // 2):
        shift = shift_of(table, core, i)
        for half, d in held:

            @pl.when(shift == d)
            def _(half=half, i=i):
                copy(half, i, near)

            @pl.when(shift - 8 == d)
            def _(half=half, i=i):
                copy(half, i, far)


def pages_of(table, own, halves, after):
    return pl.pallas_call(
        pages_kernel,
        name="pages",
        in_specs=[smem()] + [whole()] * 9 + [anywhere()],
        out_specs=[whole()] * 2,
        out_shape=[jax.ShapeDtypeStruct((PAGES_DEV // 2 * SLOT, 128), BF16)] * 2,
        compiler_params=params(16),
    )(table, own, *halves, after)


def choose_kernel(table, near, far, out):
    _, _, core = place_of()
    for i in range(PAGES_DEV // 2):
        rows = slice(i * SLOT, (i + 1) * SLOT)
        away = shift_of(table, core, i) > 8

        @pl.when(away)
        def _(rows=rows):
            out[rows, :] = far[rows, :]

        @pl.when(jnp.logical_not(away))
        def _(rows=rows):
            out[rows, :] = near[rows, :]


def choose(table, near, far):
    return pl.pallas_call(
        choose_kernel,
        name="choose",
        in_specs=[smem(), whole(), whole()],
        out_specs=whole(),
        out_shape=jax.ShapeDtypeStruct(near.shape, BF16),
        compiler_params=params(8),
    )(table, near, far)


def cache_kernel(own, came, out):
    _, _, core = place_of()
    tok = out.shape[1]
    for half, ref in ((core, own), (1 - core, came)):
        for i in range(PAGES_DEV // 2):
            at = pl.multiple_of(half * (tok // 2) + i * PAGE, PAGE)
            for g in range(GROUPS + 1):
                rows = slice(i * SLOT + g * PAGE, i * SLOT + (g + 1) * PAGE)
                page = ref[rows, :].astype(F32).T
                keep = min(PAGE, RANK + ROPE - g * PAGE)
                out[g * PAGE : g * PAGE + keep, pl.ds(at, PAGE)] = page[:keep].astype(BF16)


def cache_of(own, came, tok):
    return pl.pallas_call(
        cache_kernel,
        name="cache",
        in_specs=[whole(), whole()],
        out_specs=whole(),
        out_shape=jax.ShapeDtypeStruct((RANK + ROPE, tok), BF16),
        compiler_params=params(16),
    )(own, came).T


def on_device(
    prompt_states, decode_states, lengths, page_table, w_query, w_down, kv_gain, w_up, w_out
):
    n_ctx, n_head = lax.axis_size("ctx"), lax.axis_size("head")

    def over_ctx(block, dist_of):
        route = [
            (c * n_head + j, (c + dist_of(j)) % n_ctx * n_head + j)
            for c in range(n_ctx)
            for j in range(n_head)
        ]
        return lax.ppermute(block, ("ctx", "head"), route)

    def over_x(block, s):
        return lax.ppermute(block, "head", [(j, (j + 2 * s) % n_head) for j in range(n_head)])

    def to_sibling(block):
        return lax.ppermute(block, "head", [(j, j ^ 1) for j in range(n_head)])

    def chip_dist(j, k=0):
        return DIST[(j // 2 + k) % len(DIST)]

    gain = kv_gain[None, :]
    w_down_t = w_down.T
    w_up_sib = to_sibling(w_up)
    w_out_sib = to_sibling(w_out)
    half = latent_of(lengths, prompt_states, w_down_t, gain)
    near0 = over_ctx(half, chip_dist)
    half_sib = to_sibling(half)
    q_own = query_of(lengths, prompt_states, w_query, half_sib)
    q_sib = to_sibling(q_own)
    far0 = over_ctx(near0, lambda j: 4)
    near2 = over_ctx(near0, lambda j: chip_dist(j, 2) - chip_dist(j))
    near3 = over_x(near0, 1)
    near1 = over_x(near0, -1)
    far2 = over_ctx(far0, lambda j: chip_dist(j, 2) - chip_dist(j))
    far3 = over_x(far0, 1)
    far1 = over_x(far0, -1)

    dpart, dself = decode_partial(
        n_ctx, lengths, decode_states, w_query, w_down_t, gain, w_up, half, half_sib
    )
    parts = lax.all_to_all(dpart, "ctx", 0, 0, tiled=True)

    weights = (q_own, q_sib, w_up, w_up_sib)
    state = attend("first", lengths, *weights, [half, near0], (None, (0, 0)), [dpart])
    dec = decode_merge(parts, dself, w_out, dself)
    state = attend(
        "middle",
        lengths,
        *weights,
        [near2, near3, near1, far0],
        ((2, 0), (3, 0), (1, 0), (0, 4)),
        (*state, dpart),
    )
    mine, other = attend(
        "last", lengths, *weights, [far2, far3, far1], ((2, 4), (3, 4), (1, 4)), (*state, dec)
    )
    came = to_sibling(other)
    halves = [near0, near1, near2, near3, far0, far1, far2, far3]
    page_near, page_far = pages_of(page_table, half, halves, mine)
    out0, out1, out2, out3 = merge_out(mine, came, w_out, w_out_sib, dec, page_near)
    got1 = over_x(out1, 1)
    got3 = over_x(out3, -1)
    got2 = over_x(out2, 2)
    prefill_out, dec = sum_parts(out0, got1, got2, got3)
    decode_out = (dec + to_sibling(dec))[: decode_states.shape[0]].astype(BF16)

    page = choose(page_table, page_near, over_ctx(page_far, lambda j: 8))
    paged_cache = cache_of(page, to_sibling(page), prompt_states.shape[0])
    return (prefill_out, paged_cache, decode_out)


def solution(mesh):
    in_specs = (
        P("ctx", None),
        P(),
        P(),
        P(),
        P(None, "head"),
        P(),
        P(),
        P(None, "head"),
        P("head", None),
    )
    out_specs = (P(("ctx", "head"), None), P("ctx", None), P())
    return jax.shard_map(
        on_device, mesh=mesh, in_specs=in_specs, out_specs=out_specs, check_vma=False
    )
```

```python
import functools
import math

import jax
import jax.numpy as jnp
import numpy as np
from jax import lax
from jax.experimental import pallas as pl
from jax.experimental.pallas import tpu as pltpu
from jax.sharding import PartitionSpec as P

NOPE = 128
ROPE = 64
VDIM = 128
RANK = 512
PAGE = 128
PAGES_DEV = 4
ROPE_BASE = 50000.0
HIDDEN = -3e38
FLOOR = -1e30
KAPPA = (NOPE + ROPE) ** -0.5 * math.log2(math.e)
DIST = (1, 3, 2, 4)
FREQ = (
    ROPE_BASE ** (-(np.arange(ROPE // 2, dtype=np.float64) * 2.0 / ROPE))
).astype(np.float32)[:, None]
ATTEND_MIB = {"first": 16, "last": 24}
COST = {"first": 1 << 20, "last": 8 << 30}
EXTRA = 8

F32 = jnp.float32
BF16 = jnp.bfloat16
NT = (((1,), (1,)), ((), ()))


def whole():
    return pl.BlockSpec()


def smem():
    return pl.BlockSpec(memory_space=pltpu.SMEM)


def anywhere():
    return pl.BlockSpec(memory_space=pl.ANY)


def in_hbm(x):
    return pltpu.with_memory_space_constraint(x, pltpu.HBM)


def params(mib):
    return pltpu.CompilerParams(vmem_limit_bytes=mib << 20)


def place_of():
    head = lax.axis_index("head")
    return lax.axis_index("ctx"), head // 2, lax.rem(head, 2)


def back_of(chip):
    chip = lax.rem(chip, 4)
    return jnp.where(chip == 0, 1, jnp.where(chip == 1, 3, jnp.where(chip == 2, 2, 4)))


GROUPS = RANK // 128


def tokens_of(ref):
    return ref.shape[0] * 128 // (RANK + ROPE)


def halves_of(pairs):
    n = pairs[0].shape[0] // 2
    return [p.at[pl.ds(i * n, n)] for p in pairs for i in range(2)]


def latent_rows(ref):
    n = tokens_of(ref)
    return jnp.concatenate([ref[g * n : (g + 1) * n, :] for g in range(GROUPS)], 1)


def rotary_rows(ref):
    both = ref[GROUPS * tokens_of(ref) :, :]
    return jnp.concatenate([both[:, :ROPE], both[:, ROPE:]], 0)


def ends_of(lengths):
    e0 = lengths[0]
    e1 = e0 + lengths[1]
    return e0, e1, e1 + lengths[2]


def start_of(index, ends):
    e0, e1, e2 = ends
    return jnp.where(
        index >= e2, e2, jnp.where(index >= e1, e1, jnp.where(index >= e0, e0, 0))
    )


def normed(comp, gain):
    return comp * lax.rsqrt(jnp.mean(comp * comp, -1, keepdims=True) + 1e-06) * gain


def turn_table(place, freq):
    angle = freq * place
    cos, sin = jnp.cos(angle), jnp.sin(angle)
    return jnp.concatenate([cos, cos, -sin, sin], 0).T


def turned(v, cs):
    half = ROPE // 2
    other = jnp.concatenate([v[:, half:], v[:, :half]], 1)
    return v * cs[:, :ROPE] + other * cs[:, ROPE:]


def prompt_turns(lengths, freq, first, n):
    index = first + lax.broadcasted_iota(jnp.int32, (1, n), 1)
    place = (index - start_of(index, ends_of(lengths))).astype(F32)
    return turn_table(place, freq)


def latent_kernel(lengths, x, w, gain, freq, out, cs, acc):
    step = pl.program_id(0)
    n = x.shape[0]

    @pl.when(step == 0)
    def _():
        ctx, _, core = place_of()
        cs[...] = prompt_turns(lengths, freq[...], (2 * ctx + core) * n, n)

    part = lax.dot_general(x[...], w[...], NT, preferred_element_type=F32)

    @pl.when(step == 0)
    def _():
        acc[...] = part

    @pl.when(step > 0)
    def _():
        acc[...] += part

    @pl.when(step == pl.num_programs(0) - 1)
    def _():
        comp = normed(acc[:, :RANK], gain[...]).astype(BF16)
        for g in range(GROUPS):
            out[g * n : (g + 1) * n, :] = comp[:, g * 128 : (g + 1) * 128]
        rot = turned(acc[:, RANK:], cs[...]).astype(BF16)
        out[GROUPS * n :, :] = jnp.concatenate([rot[: n // 2], rot[n // 2 :]], 1)


def latent_of(lengths, x, w_down_t, gain):
    tok, d = x.shape
    n = tok // 2
    width = w_down_t.shape[0]
    steps = 2
    return pl.pallas_call(
        latent_kernel,
        name="latent",
        grid=(steps,),
        in_specs=[
            smem(),
            pl.BlockSpec((n, d // steps), lambda i: (lax.rem(lax.axis_index("head"), 2), i)),
            pl.BlockSpec((width, d // steps), lambda i: (0, i)),
            pl.BlockSpec((1, RANK), lambda i: (0, 0)),
            pl.BlockSpec((ROPE // 2, 1), lambda i: (0, 0)),
        ],
        out_specs=pl.BlockSpec((n * width // 128, 128), lambda i: (0, 0)),
        out_shape=jax.ShapeDtypeStruct((n * width // 128, 128), BF16),
        scratch_shapes=[pltpu.VMEM((n, 2 * ROPE), F32), pltpu.VMEM((n, width), F32)],
        compiler_params=params(60),
        cost_estimate=pl.CostEstimate(
            flops=2 * n * d * width, bytes_accessed=4 << 20, transcendentals=0
        ),
    )(lengths, in_hbm(x), in_hbm(w_down_t), gain, FREQ)


def after_kernel(x, _, out):
    pass


def passed(x, after):
    return pl.pallas_call(
        after_kernel,
        name="passed",
        in_specs=[anywhere()] * 2,
        out_specs=anywhere(),
        out_shape=jax.ShapeDtypeStruct(x.shape, x.dtype),
        input_output_aliases={0: 0},
        compiler_params=params(4),
    )(x, after)


def first_part_kernel(x, out, sem):
    copy = pltpu.make_async_copy(x, out.at[pl.ds(0, x.shape[0])], sem)
    copy.start()
    copy.wait()


def second_part_kernel(x, _, out, sem):
    copy = pltpu.make_async_copy(x, out.at[pl.ds(x.shape[0], x.shape[0])], sem)
    copy.start()
    copy.wait()


def first_part(x):
    return pl.pallas_call(
        first_part_kernel,
        name="first_part",
        in_specs=[anywhere()],
        out_specs=anywhere(),
        out_shape=jax.ShapeDtypeStruct((2 * x.shape[0], x.shape[1]), x.dtype),
        scratch_shapes=[pltpu.SemaphoreType.DMA],
        compiler_params=params(4),
    )(x)


def second_part(x, both):
    return pl.pallas_call(
        second_part_kernel,
        name="second_part",
        in_specs=[anywhere()] * 2,
        out_specs=anywhere(),
        out_shape=jax.ShapeDtypeStruct(both.shape, both.dtype),
        scratch_shapes=[pltpu.SemaphoreType.DMA],
        input_output_aliases={1: 0},
        compiler_params=params(4),
    )(x, both)


def query_kernel(lengths, x, w, freq, _, out, cs, acc):
    step = pl.program_id(0)
    tok = x.shape[0]

    @pl.when(step == 0)
    def _():
        ctx, _, _ = place_of()
        cs[...] = prompt_turns(lengths, freq[...], ctx * tok, tok)

    part = jnp.dot(x[...], w[...], preferred_element_type=F32)

    @pl.when(step == 0)
    def _():
        acc[...] = part

    @pl.when(step > 0)
    def _():
        acc[...] += part

    @pl.when(step == pl.num_programs(0) - 1)
    def _():
        for h in range(2):
            at = h * (NOPE + ROPE)
            out[h, :, :NOPE] = (acc[:, at : at + NOPE] * KAPPA).astype(BF16)
            r = turned(acc[:, at + NOPE : at + NOPE + ROPE], cs[...]) * KAPPA
            out[h, :, NOPE:] = jnp.concatenate([r, jnp.zeros_like(r)], 1).astype(BF16)


def query_of(lengths, x, w_query, after):
    tok, d = x.shape
    width = w_query.shape[1]
    steps = 2
    return pl.pallas_call(
        query_kernel,
        name="query",
        grid=(steps,),
        in_specs=[
            smem(),
            pl.BlockSpec((tok, d // steps), lambda i: (0, i)),
            pl.BlockSpec((d // steps, width), lambda i: (i, 0)),
            pl.BlockSpec((ROPE // 2, 1), lambda i: (0, 0)),
            anywhere(),
        ],
        out_specs=pl.BlockSpec((2, tok, 256), lambda i: (0, 0, 0)),
        out_shape=jax.ShapeDtypeStruct((2, tok, 256), BF16),
        scratch_shapes=[pltpu.VMEM((tok, 2 * ROPE), F32), pltpu.VMEM((tok, width), F32)],
        compiler_params=params(14),
        cost_estimate=pl.CostEstimate(
            flops=1 << 20, bytes_accessed=1 << 16, transcendentals=0
        ),
    )(lengths, in_hbm(x), in_hbm(w_query), FREQ, after)


def decode_kernel(lengths, x, w_query, w_down_t, gain, freq, w_up, half, sib, out, self_out):
    n = tokens_of(half)
    tok = 2 * n
    rows = x.shape[0]
    keys = jnp.concatenate([latent_rows(half), latent_rows(sib)], 0)
    rot = jnp.concatenate([rotary_rows(half), rotary_rows(sib)], 0)
    ctx, _, core = place_of()
    lane = lax.broadcasted_iota(jnp.int32, (1, 128), 1)
    place = jnp.zeros((1, 128), jnp.int32)
    for r in range(rows):
        place = jnp.where(lane == r, lengths[r], place)
    cs = turn_table(place.astype(F32), freq[...])[:rows]
    lat = lax.dot_general(x[...], w_down_t[...], NT, preferred_element_type=F32)
    new_c = normed(lat[:, :RANK], gain[...]).astype(BF16)
    new_k = turned(lat[:, RANK:], cs).astype(BF16)
    q = jnp.dot(x[...], w_query[...], preferred_element_type=F32)
    index = lax.broadcasted_iota(jnp.int32, (rows, tok), 1)
    index = ctx * tok + jnp.where(index < n, index + core * n, index - core * n)
    tenant = sum((index >= e).astype(jnp.int32) for e in ends_of(lengths))
    mask = tenant == lax.broadcasted_iota(jnp.int32, (rows, tok), 0)
    for h in range(2):
        at = h * (NOPE + ROPE)
        wk = w_up[:, h * 256 : h * 256 + NOPE]
        wv = w_up[:, h * 256 + NOPE : h * 256 + 256]
        qn = (q[:, at : at + NOPE] * KAPPA).astype(BF16)
        qa = lax.dot_general(qn, wk, NT, preferred_element_type=F32).astype(BF16)
        qr = (turned(q[:, at + NOPE : at + NOPE + ROPE], cs) * KAPPA).astype(BF16)
        s = lax.dot_general(qa, keys, NT, preferred_element_type=F32)
        s = s + lax.dot_general(qr, rot, NT, preferred_element_type=F32)
        s = jnp.where(mask, s, HIDDEN)
        top = jnp.maximum(jnp.max(s, -1, keepdims=True), FLOOR)
        p = jnp.exp2(s - top)
        total = jnp.sum(p, -1, keepdims=True)
        mixed = jnp.dot(p.astype(BF16), keys, preferred_element_type=F32)
        part = jnp.dot(mixed.astype(BF16), wv, preferred_element_type=F32)
        own = jnp.sum(qa.astype(F32) * new_c.astype(F32), -1, keepdims=True)
        own = own + jnp.sum(qr.astype(F32) * new_k.astype(F32), -1, keepdims=True)
        to = slice(h * rows, h * rows + rows)
        mine = jnp.concatenate(
            [part, jnp.broadcast_to(top, (rows, 64)), jnp.broadcast_to(total, (rows, 64))], 1
        )
        for c in range(out.shape[0] // (2 * rows)):
            at = c * 2 * rows + h * rows
            out[at : at + rows, :] = mine
        self_out[to, :VDIM] = jnp.dot(new_c, wv, preferred_element_type=F32)
        self_out[to, VDIM : VDIM + 64] = jnp.broadcast_to(own, (rows, 64))
        self_out[to, VDIM + 64 :] = jnp.ones((rows, 64), F32)


def decode_partial(copies, lengths, x, w_query, w_down_t, gain, w_up, half, sib):
    rows = x.shape[0]
    return pl.pallas_call(
        decode_kernel,
        name="decode_partial",
        in_specs=[smem()] + [whole()] * 8,
        out_specs=[whole()] * 2,
        out_shape=[
            jax.ShapeDtypeStruct((copies * 2 * rows, 256), F32),
            jax.ShapeDtypeStruct((2 * rows, 256), F32),
        ],
        compiler_params=params(12),
        cost_estimate=pl.CostEstimate(
            flops=1 << 20, bytes_accessed=1 << 16, transcendentals=0
        ),
    )(lengths, x, w_query, w_down_t, gain, FREQ, w_up, half, sib)


def decode_merge_kernel(parts, own, w_out, _, out):
    rows = own.shape[0] // 2
    n = parts.shape[0] // own.shape[0]
    part = [parts[i * 2 * rows : (i + 1) * 2 * rows, :] for i in range(n)] + [own[...]]
    tops = [p[:, VDIM : VDIM + 1] for p in part]
    top = functools.reduce(jnp.maximum, tops)
    ratio = [jnp.exp2(t - top) for t in tops]
    total = sum(r * p[:, VDIM + 64 : VDIM + 65] for r, p in zip(ratio, part))
    acc = sum(r * p[:, :VDIM] for r, p in zip(ratio, part))
    heads = (acc / total).astype(BF16)
    got = jnp.dot(heads[:rows], w_out[:VDIM], preferred_element_type=F32)
    got = got + jnp.dot(heads[rows:], w_out[VDIM:], preferred_element_type=F32)
    out[...] = jnp.concatenate([got, jnp.zeros((EXTRA - rows, got.shape[1]), F32)], 0)


def decode_merge(parts, own, w_out, after):
    return pl.pallas_call(
        decode_merge_kernel,
        name="decode_merge",
        in_specs=[whole()] * 3 + [anywhere()],
        out_specs=whole(),
        out_shape=jax.ShapeDtypeStruct((EXTRA, w_out.shape[1]), F32),
        compiler_params=params(4),
        cost_estimate=pl.CostEstimate(
            flops=2 * 8 * 2048 * 256, bytes_accessed=2 << 20, transcendentals=0
        ),
    )(parts, own, w_out, after)


def attend_kernel(stage, places, lengths, q_own, q_sib, w_own, w_sib, *refs):
    segs, refs = refs[:3], refs[3:]
    if stage == "first":
        _, acc_out, rbuf, kbuf, vbuf, sbuf = refs
    else:
        acc_in, _, mine, other, rbuf, kbuf, vbuf, sbuf, tile = refs
        segs = halves_of(segs)
    tok = q_own.shape[1]
    heads = 4
    ctx, chip, core = place_of()
    base = ctx * tok
    ends = ends_of(lengths)
    row = base + lax.broadcasted_iota(jnp.int32, (tok, 128), 0)
    low = start_of(row, ends)
    blocks = []
    at = 0
    n = tokens_of(segs[0])
    for lat, place in zip(segs, places):
        if place is None:
            back = base + core * n
        else:
            back = base + core * n - (back_of(chip + place[0]) + place[1]) * tok
        rot = rotary_rows(lat)
        rbuf[at : at + n, :] = jnp.concatenate([rot, jnp.zeros_like(rot)], 1)
        blocks.append((lat, at, back, place is None))
        at += n
    ones = jnp.ones((n, 256 - VDIM), BF16)

    def expand(h):
        w = (w_own if h < 2 else w_sib)[:, (h % 2) * 256 : (h % 2) * 256 + 256]
        for lat, at, _, _ in blocks:
            kv = jnp.dot(latent_rows(lat), w, preferred_element_type=F32)
            kbuf[h, at : at + n, :] = kv[:, :NOPE].astype(BF16)
            vbuf[h, at : at + n, :] = kv[:, NOPE:].astype(BF16)

    def scores(h, block, top):
        _, at, back, causal = block
        q = q_own[h] if h < 2 else q_sib[h - 2]
        k = jnp.concatenate([kbuf[h, at : at + n, :], rbuf[at : at + n, :]], 1)
        s = lax.dot_general(q, k, NT, preferred_element_type=F32)
        for g in range(0, n, 128):
            key = back + g + lax.broadcasted_iota(jnp.int32, (1, 128), 1)
            mask = key >= low
            if causal:
                mask = mask & (key <= row)
            piece = jnp.where(mask, s[:, g : g + 128], HIDDEN)
            sbuf[h % 2, :, at + g : at + g + 128] = piece
            top = piece if top is None else jnp.maximum(top, piece)
        return top

    def finish(h, top, acc):
        if stage != "last":
            acc_out[h, :, : VDIM + 64] = acc[:, : VDIM + 64]
            acc_out[h, :, VDIM + 64 :] = jnp.broadcast_to(top, (tok, 64))
            return
        total = acc[:, VDIM:]
        some = total > 0
        safe = jnp.where(some, total, 1.0)
        tile[:, h * VDIM : h * VDIM + VDIM] = acc[:, :VDIM] / safe
        lse = jnp.where(some, top + jnp.log2(safe), HIDDEN)
        lane = lax.broadcasted_iota(jnp.int32, (tok, 128), 1)
        if h == 0:
            tile[:, heads * VDIM :] = lse
        else:
            tile[:, heads * VDIM :] = jnp.where(
                lane // 32 == h, lse, tile[:, heads * VDIM :]
            )

    expand(0)
    tops = None
    for block in blocks:
        tops = scores(0, block, tops)
    for h in range(heads):
        top = jnp.max(tops, -1, keepdims=True)
        tops = None
        if stage == "first":
            top = jnp.maximum(top, FLOOR)
            acc = None
        else:
            before = acc_in[h, :, VDIM + 64 : VDIM + 65]
            top = jnp.maximum(top, before)
            ratio = jnp.exp2(before - top)
            total = acc_in[h, :, VDIM : VDIM + 1] * ratio
            acc = jnp.concatenate(
                [acc_in[h, :, :VDIM] * ratio, jnp.broadcast_to(total, (tok, VDIM))], 1
            )
        if h + 1 < heads:
            expand(h + 1)
        for block in blocks:
            _, at, _, _ = block
            if h + 1 < heads:
                tops = scores(h + 1, block, tops)
            p = jnp.exp2(sbuf[h % 2, :, at : at + n] - top).astype(BF16)
            v = jnp.concatenate([vbuf[h, at : at + n, :], ones], 1)
            got = jnp.dot(p, v, preferred_element_type=F32)
            acc = got if acc is None else acc + got
        finish(h, top, acc)
    if stage == "last":
        part = tok // 8
        for i in range(4):
            to = slice(i * part, (i + 1) * part)
            at = (2 * i + core) * part
            mine[to, :] = tile[pl.ds(pl.multiple_of(at, part), part), :]
            at = (2 * i + 1 - core) * part
            other[to, :] = tile[pl.ds(pl.multiple_of(at, part), part), :]


def attend(stage, lengths, q_own, q_sib, w_own, w_sib, segs, places, state):
    _, tok, _ = q_own.shape
    heads = 4
    keys = tok // 2 * len(places)
    args = [lengths, q_own, q_sib, w_own, w_sib, *segs, *state]
    scratch = [
        pltpu.VMEM((keys, 128), BF16),
        pltpu.VMEM((heads, keys, 128), BF16),
        pltpu.VMEM((heads, keys, 128), BF16),
        pltpu.VMEM((2, tok, keys), F32),
    ]
    if stage == "last":
        width = heads * VDIM + 128
        out_shape = [jax.ShapeDtypeStruct((tok // 2, width), F32)] * 2
        scratch.append(pltpu.VMEM((tok, width), F32))
    else:
        out_shape = [jax.ShapeDtypeStruct((heads, tok, 256), F32)]
    return pl.pallas_call(
        functools.partial(attend_kernel, stage, places),
        name="attend_" + stage,
        in_specs=[smem()] + [whole()] * (len(args) - 2) + [anywhere()],
        out_specs=[whole()] * len(out_shape),
        out_shape=out_shape,
        scratch_shapes=scratch,
        compiler_params=params(ATTEND_MIB[stage]),
        cost_estimate=pl.CostEstimate(
            flops=COST[stage],
            bytes_accessed=1 << 16,
            transcendentals=0,
        ),
    )(*args)


def merge_kernel(mine, came, w_own, w_sib, dec, dec_sib, _, out0, out1, out2, out3, heads):
    _, chip, _ = place_of()
    wide = 4 * VDIM
    for h in range(4):
        g = (h + 2) % 4
        la = mine[:, wide + h * 32 : wide + h * 32 + 1]
        lb = came[:, wide + g * 32 : wide + g * 32 + 1]
        top = jnp.maximum(la, lb)
        wa, wb = jnp.exp2(la - top), jnp.exp2(lb - top)
        scale = 1.0 / (wa + wb)
        o = mine[:, h * VDIM : h * VDIM + VDIM] * (wa * scale)
        o = o + came[:, g * VDIM : g * VDIM + VDIM] * (wb * scale)
        heads[:, h * VDIM : h * VDIM + VDIM] = o.astype(BF16)
    quarter = heads.shape[0] // 4
    part = jnp.concatenate(
        [
            heads[pl.ds(pl.multiple_of(lax.rem(chip + i, 4) * quarter, quarter), quarter), :]
            for i in range(4)
        ],
        0,
    )
    got = jnp.dot(part[:, : 2 * VDIM], w_own[...], preferred_element_type=F32)
    got = got + jnp.dot(part[:, 2 * VDIM :], w_sib[...], preferred_element_type=F32)
    both = dec[...]
    wide = both.shape[1] // 2
    packed = jnp.concatenate(
        [
            jnp.concatenate([both[:4, g : g + 128], both[:4, wide + g : wide + g + 128]], 0)
            for g in range(0, wide, 128)
        ],
        0,
    )
    parts = [
        jnp.concatenate([got[i * quarter : (i + 1) * quarter], packed], 1) for i in range(4)
    ]
    out0[...] = parts[0]
    out1[...] = parts[1].astype(BF16)
    out2[...] = parts[2].astype(BF16)
    out3[...] = parts[3].astype(BF16)


def merge_out(mine, came, w_own, w_sib, dec, dec_sib, after):
    rows, d = mine.shape[0], w_own.shape[1]
    shapes = [jax.ShapeDtypeStruct((rows // 4, d + 128), F32)]
    shapes += [jax.ShapeDtypeStruct((rows // 4, d + 128), BF16)] * 3
    return pl.pallas_call(
        merge_kernel,
        name="merge_out",
        in_specs=[whole()] * 6 + [anywhere()],
        out_specs=[whole()] * 4,
        out_shape=shapes,
        scratch_shapes=[pltpu.VMEM((rows, 4 * VDIM), BF16)],
        compiler_params=params(24),
        cost_estimate=pl.CostEstimate(
            flops=2 * rows * 512 * d, bytes_accessed=5 << 20, transcendentals=0
        ),
    )(mine, came, w_own, w_sib, dec, dec_sib, after)


def sum_kernel(own, a, b, c, out, dec):
    rows = out.shape[0]
    got = own[...] + a[...].astype(F32) + b[...].astype(F32) + c[...].astype(F32)
    d = out.shape[1]
    out[...] = got[:, :d].astype(BF16)
    for i in range(rows // 8):
        piece = got[8 * i : 8 * i + 8, d:]
        dec[:, 128 * i : 128 * i + 128] = piece[:4]
        dec[:, d // 2 + 128 * i : d // 2 + 128 * i + 128] = piece[4:]


def sum_parts(own, a, b, c, requests):
    rows, d = own.shape[0], own.shape[1] - 128
    return pl.pallas_call(
        sum_kernel,
        name="sum_parts",
        in_specs=[whole()] * 4,
        out_specs=[whole()] * 2,
        out_shape=[
            jax.ShapeDtypeStruct((rows, d), BF16),
            jax.ShapeDtypeStruct((requests, d), F32),
        ],
        compiler_params=params(16),
        cost_estimate=pl.CostEstimate(
            flops=40_000_000_000, bytes_accessed=2 << 20, transcendentals=0
        ),
    )(own, a, b, c)


SLOT = RANK + PAGE


def shift_of(table, core, i):
    at = lax.div(table[2 * core + i], PAGES_DEV)
    return at


def pages_kernel(table, own, *refs):
    near0, far0, *pairs, _, near, far = refs
    _, chip, core = place_of()
    held = [(own, 0)]
    for i, half in enumerate([near0, far0] + halves_of(pairs)):
        held.append((half, back_of(chip + i // 2) + i % 2 * 4))

    def copy(half, i, out):
        n = tokens_of(half)
        for g in range(GROUPS):
            at = g * n + i * PAGE
            out[i * SLOT + g * PAGE : i * SLOT + (g + 1) * PAGE, :] = half[at : at + PAGE, :]
        rot = half[GROUPS * n :, :]
        if i:
            rot = jnp.concatenate([rot[:, ROPE:], rot[:, :ROPE]], 1)
        out[i * SLOT + RANK : (i + 1) * SLOT, :] = rot

    for i in range(PAGES_DEV // 2):
        shift = shift_of(table, core, i)
        for half, d in held:

            @pl.when(shift == d)
            def _(half=half, i=i):
                copy(half, i, near)

            @pl.when(shift - 8 == d)
            def _(half=half, i=i):
                copy(half, i, far)


def pages_of(table, own, halves, after):
    return pl.pallas_call(
        pages_kernel,
        name="pages",
        in_specs=[smem()] + [whole()] * 6 + [anywhere()],
        out_specs=[whole()] * 2,
        out_shape=[jax.ShapeDtypeStruct((PAGES_DEV // 2 * SLOT, 128), BF16)] * 2,
        compiler_params=params(16),
    )(table, own, *halves, after)


def choose_kernel(table, near, far, out):
    _, _, core = place_of()
    for i in range(PAGES_DEV // 2):
        rows = slice(i * SLOT, (i + 1) * SLOT)
        away = shift_of(table, core, i) > 8

        @pl.when(away)
        def _(rows=rows):
            out[rows, :] = far[rows, :]

        @pl.when(jnp.logical_not(away))
        def _(rows=rows):
            out[rows, :] = near[rows, :]


def choose(table, near, far):
    return pl.pallas_call(
        choose_kernel,
        name="choose",
        in_specs=[smem(), whole(), whole()],
        out_specs=whole(),
        out_shape=jax.ShapeDtypeStruct(near.shape, BF16),
        compiler_params=params(8),
    )(table, near, far)


def cache_kernel(own, came, out):
    _, _, core = place_of()
    tok = out.shape[1]
    for half, ref in ((core, own), (1 - core, came)):
        for i in range(PAGES_DEV // 2):
            at = pl.multiple_of(half * (tok // 2) + i * PAGE, PAGE)
            for g in range(GROUPS + 1):
                rows = slice(i * SLOT + g * PAGE, i * SLOT + (g + 1) * PAGE)
                page = ref[rows, :].astype(F32).T
                keep = min(PAGE, RANK + ROPE - g * PAGE)
                out[g * PAGE : g * PAGE + keep, pl.ds(at, PAGE)] = page[:keep].astype(BF16)


def cache_of(own, came, tok):
    return pl.pallas_call(
        cache_kernel,
        name="cache",
        in_specs=[whole(), whole()],
        out_specs=whole(),
        out_shape=jax.ShapeDtypeStruct((RANK + ROPE, tok), BF16),
        compiler_params=params(16),
    )(own, came)


def on_device(
    prompt_states, decode_states, lengths, page_table, w_query, w_down, kv_gain, w_up, w_out
):
    n_ctx, n_head = lax.axis_size("ctx"), lax.axis_size("head")

    def over_ctx(block, dist_of):
        route = [
            (c * n_head + j, (c + dist_of(j)) % n_ctx * n_head + j)
            for c in range(n_ctx)
            for j in range(n_head)
        ]
        return lax.ppermute(block, ("ctx", "head"), route)

    def over_x(block, s):
        return lax.ppermute(block, "head", [(j, (j + 2 * s) % n_head) for j in range(n_head)])

    def to_sibling(block):
        return lax.ppermute(block, "head", [(j, j ^ 1) for j in range(n_head)])

    def chip_dist(j, k=0):
        return DIST[(j // 2 + k) % len(DIST)]

    gain = kv_gain[None, :]
    w_down_t = w_down.T
    w_up_sib = to_sibling(w_up)
    w_out_sib = to_sibling(w_out)
    half = latent_of(lengths, prompt_states, w_down_t, gain)
    near0 = over_ctx(half, chip_dist)
    half_sib = to_sibling(half)

    dpart, dself = decode_partial(
        n_ctx, lengths, decode_states, w_query, w_down_t, gain, w_up, half, half_sib
    )
    parts = lax.all_to_all(dpart, "ctx", 0, 0, tiled=True)

    q_own = query_of(lengths, prompt_states, w_query, parts)
    q_sib = to_sibling(q_own)
    near0 = passed(near0, dpart)
    far0 = over_ctx(near0, lambda j: 4)
    pair0 = second_part(far0, first_part(near0))
    pair3 = over_x(pair0, 1)
    pair1 = over_x(pair0, -1)
    pair2 = over_ctx(pair0, lambda j: chip_dist(j, 2) - chip_dist(j))

    weights = (q_own, q_sib, w_up, w_up_sib)
    state = attend(
        "first", lengths, *weights, [half, near0, far0], (None, (0, 0), (0, 4)), [dself]
    )
    dec = decode_merge(parts, dself, w_out, dself)
    mine, other = attend(
        "last",
        lengths,
        *weights,
        [pair1, pair2, pair3],
        ((1, 0), (1, 4), (2, 0), (2, 4), (3, 0), (3, 4)),
        (*state, dec),
    )
    came = to_sibling(other)
    page_near, page_far = pages_of(page_table, half, [near0, far0, pair1, pair2, pair3], mine)
    out0, out1, out2, out3 = merge_out(mine, came, w_out, w_out_sib, dec, dec, page_near)
    got2 = over_x(out2, 2)
    got1 = over_x(out1, 1)
    got3 = over_x(out3, -1)

    page = choose(page_table, page_near, over_ctx(page_far, lambda j: 8))
    cache_t = cache_of(page, to_sibling(page), prompt_states.shape[0])
    prefill_out, decode_out = sum_parts(
        out0, got1, got2, got3, decode_states.shape[0]
    )
    decode_out = (decode_out + to_sibling(decode_out)).astype(BF16)
    return (prefill_out, cache_t.T, decode_out)


def solution(mesh):
    in_specs = (
        P("ctx", None),
        P(),
        P(),
        P(),
        P(None, "head"),
        P(),
        P(),
        P(None, "head"),
        P("head", None),
    )
    out_specs = (P(("ctx", "head"), None), P("ctx", None), P())
    return jax.shard_map(
        on_device, mesh=mesh, in_specs=in_specs, out_specs=out_specs, check_vma=False
    )
```
